32 devices in a mesh: groups: 2 (over y), row: 16 (over z, x, core).
Axes of the slice: x: 2, y: 2, z: 4, core: 2. Of those that a mesh axis runs over, the one named last changes fastest.
Arguments:
- homolog_activation: float32 [32, 512, 256], P('groups', 'row'), parts along dimension 0, may hold values from -6 to 6
- homolog_entry_valid: int32 [32, 512], P('groups', 'row'), parts along dimension 0, may hold values 0 or 1
- amino_valid_flags: int32 [1024], P(('groups', 'row')), parts along dimension 0, may hold values 0 or 1
- first_factor_weights: float32 [256, 32], replicated, may hold values from -0.375 to 0.375
- second_factor_weights: float32 [256, 32], replicated, may hold values from -0.375 to 0.375
- final_linear_weights: float32 [1024, 128], replicated, may hold values from -0.1875 to 0.1875
- couple_delta_deriv: float32 [1024, 512, 128], P(('groups', 'row')), parts along dimension 0, may hold values from -6 to 6
Outputs:
- alignment_grad: float32 [32, 512, 256], P('groups', 'row'), parts along dimension 0
- left_weight_grad: float32 [512, 32], P('groups'), parts along dimension 0
- right_weight_grad: float32 [512, 32], P('groups'), parts along dimension 0
- out_weight_grad: float32 [2048, 128], P('groups'), parts along dimension 0
The draws below stay inside these ranges and needn't reach their ends.
There are 2 independent parts, one for each index of `groups`. The reference program is written for one: setup_inputs(seed, part) draws one part's arguments, and reference() takes and returns one part's arrays. A program takes and returns all parts, laid end to end along the dimension named above; an argument that names none is the same for every part. Nothing has to cross between parts.
All inputs are finite; a program needn't handle non-finite values. No bound on the sum of `homolog_entry_valid` or of `amino_valid_flags` on one device may be relied on, other than what follows from the above.
Results may differ from the reference program's by a relative error of at most 0.0003.
Values sent between devices are 32-bit elements; how exact they have to be, the bound alone decides.
A program may use at most 128 MiB of HBM per device.

```python
import jax
import jax.numpy as jnp
from jax import lax

FAMILY_DIMS = 256
MAPPED_DIMS = 32
PAIR_CHANNELS = 128
AMINO_NUMBER = 512
HOMOLOG_NUMBER = 16


def with_ends(entries, stream_key, least, high):
    place = [jax.random.randint(jax.random.fold_in(stream_key, axis), (), 0, length) for axis, length in enumerate(entries.shape)]
    longest = entries.shape.index(max(entries.shape))
    beside = place[:longest] + [(place[longest] + 1) % entries.shape[longest]] + place[longest + 1:]
    return entries.at[tuple(place)].set(least).at[tuple(beside)].set(high)


def raised(array, stream_key, source, target, blocks, factor):
    owner, partner = [(jnp.arange(array.shape[dim]) // (array.shape[dim] // blocks)).reshape([-1 if axis == dim else 1 for axis in range(array.ndim)]) for dim in (source, target)]
    chosen = jax.random.permutation(stream_key, blocks)[partner]
    strong = (owner == chosen) | (owner == (partner + blocks // 2) % blocks)
    return jnp.where(strong, factor * array, array)


def block_levels(key, dims, cuts, least, largest):
    def one(position, blocks):
        heights = jax.random.uniform(jax.random.fold_in(jax.random.fold_in(key, 6), position), (blocks,), jnp.float32, least / len(cuts), largest / len(cuts))
        return jnp.repeat(jnp.exp(heights), dims[position] // blocks).reshape((-1,) + (1,) * (len(dims) - position - 1))

    loudness = one(*cuts[0])
    for cut in cuts[1:]:
        loudness = loudness * one(*cut)
    return loudness


def noise(key, extent, width, reach, cuts=(), kind=jnp.bfloat16):
    result = width * jax.random.normal(key, extent, jnp.float32)
    if cuts:
        result = result * block_levels(key, extent, cuts, -0.22, 0.18)
    return jnp.clip(result, -reach, reach).astype(kind)


def heavy_noise(own_key, dims, scale, reach, shards, heavy, held_as=jnp.bfloat16):
    result = scale * jax.random.normal(own_key, dims, jnp.float32)
    if shards:
        result = result * block_levels(own_key, dims, shards, -0.22, 0.18)
    return jnp.clip(raised(result, jax.random.fold_in(own_key, 3), *heavy), -reach, reach).astype(held_as)


def setup_inputs(seed: int = 0, part: int = 0) -> dict:
    splits = jax.random.split(jax.random.key(seed), 8)
    own_keys = jax.random.split(jax.random.fold_in(splits[7], part), 8)
    homolog_activation = noise(own_keys[0], (HOMOLOG_NUMBER, AMINO_NUMBER, FAMILY_DIMS), 1.0, 6.0, ((1, 16),), jnp.float32)
    homolog_entry_valid = with_ends((jax.random.randint(own_keys[1], (HOMOLOG_NUMBER, AMINO_NUMBER), 0, 2) < 1).astype(jnp.int32), jax.random.fold_in(own_keys[1], 1), 0, 1)
    amino_valid_flags = with_ends((jax.random.randint(own_keys[2], (AMINO_NUMBER,), 0, 8) < 7).astype(jnp.int32), jax.random.fold_in(own_keys[2], 1), 0, 1)
    first_factor_weights = noise(splits[3], (FAMILY_DIMS, MAPPED_DIMS), FAMILY_DIMS ** -0.5, 0.375, (), jnp.float32)
    second_factor_weights = noise(splits[4], (FAMILY_DIMS, MAPPED_DIMS), FAMILY_DIMS ** -0.5, 0.375, (), jnp.float32)
    final_linear_weights = noise(splits[5], (MAPPED_DIMS * MAPPED_DIMS, PAIR_CHANNELS), (MAPPED_DIMS * MAPPED_DIMS) ** -0.5, 0.1875, (), jnp.float32)
    couple_delta_deriv = heavy_noise(own_keys[6], (AMINO_NUMBER, AMINO_NUMBER, PAIR_CHANNELS), 1.0, 6.0, ((0, 16),), (0, 1, 16, 2.0), jnp.float32)
    return dict(homolog_activation=homolog_activation, homolog_entry_valid=homolog_entry_valid, amino_valid_flags=amino_valid_flags, first_factor_weights=first_factor_weights, second_factor_weights=second_factor_weights, final_linear_weights=final_linear_weights, couple_delta_deriv=couple_delta_deriv)


SPLIT_PIECES = lax.Precision.HIGHEST


def reference(homolog_activation, homolog_entry_valid, amino_valid_flags, first_factor_weights, second_factor_weights, final_linear_weights, couple_delta_deriv):
    keep_mask = homolog_entry_valid.astype(jnp.float32)
    validity_swapped = keep_mask.T
    present = amino_valid_flags.astype(jnp.float32)
    first_factor_embed = jnp.einsum('gsj,ju->sgu', homolog_activation, first_factor_weights, precision=SPLIT_PIECES) * validity_swapped[:, :, None]
    second_factor_embed = jnp.einsum('gsj,ju->sgu', homolog_activation, second_factor_weights, precision=SPLIT_PIECES) * validity_swapped[:, :, None]
    count = jnp.dot(validity_swapped, keep_mask, precision=SPLIT_PIECES, preferred_element_type=jnp.float32)
    factor = present[:, None] * present[None, :] / jnp.maximum(count, 1.0)
    w_three = final_linear_weights.reshape(MAPPED_DIMS, MAPPED_DIMS, PAIR_CHANNELS)
    stride = 64
    nblocks = AMINO_NUMBER // stride

    def step(carry, index):
        right_acc, out_acc = carry
        begin = (index * stride).astype(jnp.int32)
        grads = lax.dynamic_slice_in_dim(couple_delta_deriv, begin, stride, 0)
        grads = grads * lax.dynamic_slice_in_dim(factor, begin, stride, 0)[:, :, None]
        left_blk = lax.dynamic_slice_in_dim(first_factor_embed, begin, stride, 0)
        feats = jnp.einsum('ijk,abk->ijab', grads, w_three, precision=SPLIT_PIECES)
        left_part = jnp.einsum('ijab,jsb->isa', feats, second_factor_embed, precision=SPLIT_PIECES)
        right_acc = right_acc + jnp.einsum('ijab,isa->jsb', feats, left_blk, precision=SPLIT_PIECES)
        outer = jnp.einsum('isa,jsb->ijab', left_blk, second_factor_embed, precision=SPLIT_PIECES)
        out_acc = out_acc + jnp.einsum('ijab,ijk->abk', outer, grads, precision=SPLIT_PIECES)
        return (right_acc, out_acc), left_part

    start = (jnp.zeros((AMINO_NUMBER, HOMOLOG_NUMBER, MAPPED_DIMS), jnp.float32), jnp.zeros((MAPPED_DIMS, MAPPED_DIMS, PAIR_CHANNELS), jnp.float32))
    (second_factor_embed_deriv, output_grad), parts = lax.scan(step, start, jnp.arange(nblocks, dtype=jnp.int32))
    first_factor_embed_deriv = parts.reshape(AMINO_NUMBER, HOMOLOG_NUMBER, MAPPED_DIMS) * validity_swapped[:, :, None]
    second_factor_embed_deriv = second_factor_embed_deriv * validity_swapped[:, :, None]
    alignment_grad = jnp.einsum('ztp,fp->tzf', first_factor_embed_deriv, first_factor_weights, precision=SPLIT_PIECES) + jnp.einsum('ztp,fp->tzf', second_factor_embed_deriv, second_factor_weights, precision=SPLIT_PIECES)
    first_operand_array = jnp.einsum('zea,ezi->ai', homolog_activation, first_factor_embed_deriv, precision=SPLIT_PIECES)
    second_operand_array = jnp.einsum('zea,ezi->ai', homolog_activation, second_factor_embed_deriv, precision=SPLIT_PIECES)
    return (alignment_grad, first_operand_array, second_operand_array, output_grad.reshape(MAPPED_DIMS * MAPPED_DIMS, PAIR_CHANNELS))
```

```python
import functools

import jax
import jax.numpy as jnp
from jax import lax
from jax.experimental import pallas as pl
from jax.experimental.pallas import tpu as pltpu
from jax.sharding import PartitionSpec as P

EXACT = lax.Precision.HIGHEST
F32, BF16 = jnp.float32, jnp.bfloat16
LANES = 128


def split(x):
    hi = x.astype(BF16)
    return hi, (x - hi.astype(F32)).astype(BF16)


def nn(a, b):
    return jnp.dot(a, b, preferred_element_type=F32)


def nt(a, b):
    return lax.dot_general(a, b, (((1,), (1,)), ((), ())), preferred_element_type=F32)


def remote(src, dst, send, recv, target):
    return pltpu.make_async_remote_copy(
        src_ref=src,
        dst_ref=dst,
        send_sem=send,
        recv_sem=recv,
        device_id={"row": target},
        device_id_type=pl.DeviceIdType.MESH,
    )


def places(n):
    me = lax.axis_index("row")
    return me, me + 1 - 2 * lax.rem(me, 2)


def greet(n):
    me, partner = places(n)
    barrier = pltpu.get_barrier_semaphore()
    pl.semaphore_signal(barrier, inc=1, device_id={"row": partner}, device_id_type=pl.DeviceIdType.MESH)

    def one(k, _):
        pl.semaphore_signal(
            barrier, inc=1, device_id={"row": lax.rem(me + 2 * k, n)}, device_id_type=pl.DeviceIdType.MESH
        )
        return 0

    lax.fori_loop(1, n // 2, one, 0)
    pl.semaphore_wait(barrier, n // 2)


def gather(n, own, out, send, fwd, recv):
    me, partner = places(n)
    half = n // 2

    def push(k, _):
        remote(own, out.at[me], send.at[k], recv.at[me], lax.rem(me + 2 * k, n)).start()
        return 0

    lax.fori_loop(1, half, push, 0)
    remote(own, out.at[me], send.at[0], recv.at[me], partner).start()
    out[me] = own[...]

    def relay(k, _):
        source = lax.rem(me - 2 * k + n, n)
        copy = remote(out.at[source], out.at[source], fwd.at[k], recv.at[source], partner)
        copy.wait_recv()
        copy.start()
        return 0

    lax.fori_loop(1, half, relay, 0)

    def arrive(k, _):
        source = lax.rem(partner - 2 * k + n, n)
        remote(own, out.at[source], send.at[k], recv.at[source], partner).wait_recv()
        return 0

    lax.fori_loop(0, half, arrive, 0)
    remote(own, out.at[me], send.at[0], recv.at[me], partner).wait_send()

    def sent(k, _):
        remote(own, out.at[me], send.at[k], recv.at[me], partner).wait_send()
        remote(own, out.at[me], fwd.at[k], recv.at[me], partner).wait_send()
        return 0

    lax.fori_loop(1, half, sent, 0)


def scatter_sum(n, x, near, far, staged, near_send, near_recv, far_send, far_recv):
    me, partner = places(n)
    half = n // 2

    def give(k):
        owner = lax.rem(partner + 2 * k, n)
        return remote(x.at[owner], near.at[k], near_send.at[k], near_recv.at[k], partner)

    def far_copy(k):
        return remote(staged.at[k], far.at[k], far_send.at[k], far_recv.at[k], lax.rem(me + 2 * k, n))

    def start(k, _):
        give(k).start()
        return 0

    lax.fori_loop(1, half, start, 0)
    give(0).start()

    def pair(k, _):
        give(k).wait_recv()
        staged[k] = x[lax.rem(me + 2 * k, n)] + near[k]
        far_copy(k).start()
        return 0

    lax.fori_loop(1, half, pair, 0)
    give(0).wait_recv()
    staged[0] = x[me] + near[0]

    def take(k, _):
        far_copy(k).wait_recv()
        staged[0] = staged[0] + far[k]
        return 0

    lax.fori_loop(1, half, take, 0)

    def sent(k, _):
        give(k).wait_send()
        return 0

    def far_sent(k, _):
        far_copy(k).wait_send()
        return 0

    lax.fori_loop(0, half, sent, 0)
    lax.fori_loop(1, half, far_sent, 0)
    return staged.at[0]


def gather_kernel(n, x, out, send, fwd, recv):
    greet(n)
    gather(n, x, out, send, fwd, recv)


def scatter_kernel(n, x, out, near, far, staged, *sems):
    greet(n)
    out[...] = scatter_sum(n, x, near, far, staged, *sems)[...]


def reduce_kernel(n, x, out, near, far, staged, near_send, near_recv, far_send, far_recv, send, fwd, recv):
    greet(n)
    own = scatter_sum(n, x, near, far, staged, near_send, near_recv, far_send, far_recv)
    gather(n, own, out, send, fwd, recv)


VM = pl.BlockSpec(memory_space=pltpu.VMEM)


def comm(body, n, name, ident, out_shape, scratch):
    return pl.pallas_call(
        functools.partial(body, n),
        out_shape=jax.ShapeDtypeStruct(out_shape, F32),
        in_specs=[VM],
        out_specs=VM,
        scratch_shapes=scratch,
        name=name,
        compiler_params=pltpu.CompilerParams(collective_id=ident, has_side_effects=True, vmem_limit_bytes=32 << 20),
    )


def sems(*counts):
    return [pltpu.SemaphoreType.DMA((c,)) for c in counts]


def pair_kernel(
    step,
    fam,
    cdd,
    masks,
    keep_rows,
    present_row,
    right,
    left,
    left_t,
    weights,
    right_terms,
    out_grad,
    left_grad,
    rt_hi,
    rt_lo,
    u_hi,
    u_lo,
    c_hi,
    c_lo,
):
    g = pl.program_id(0)
    width = left.shape[1]
    rows = left.shape[0] // fam
    pair = LANES

    @pl.when(g == 0)
    def _():
        hi, lo = split(right[...].T)
        rt_hi[...] = hi
        rt_lo[...] = lo
        l_hi, l_lo = split(left[...])
        l_three = jnp.concatenate([l_hi.astype(F32), l_hi.astype(F32), l_lo.astype(F32)], axis=1).astype(BF16)

        @pl.loop(0, width // 2)
        def _(q):
            lanes = pl.ds(pl.multiple_of(q * 2 * pair, 2 * pair), 2 * pair)
            w_hi, w_lo = split(weights[:, lanes])
            hi, lo = split(nn(l_three, jnp.concatenate([w_hi, w_lo, w_hi], axis=0)))
            for b in range(2):
                dest = pl.ds(pl.multiple_of((2 * q + b) * fam, fam), fam)
                for r in range(rows):
                    at = slice(r * pair, (r + 1) * pair)
                    u_hi[dest, at] = hi[r * fam : (r + 1) * fam, b * pair : (b + 1) * pair]
                    u_lo[dest, at] = lo[r * fam : (r + 1) * fam, b * pair : (b + 1) * pair]

        right_terms[...] = jnp.zeros_like(right_terms)

    count = nt(masks[...].astype(BF16), keep_rows[0].astype(BF16))
    factor = masks[:, fam : fam + 1] * present_row[0] / jnp.maximum(count, 1.0)
    s_hi, s_lo = split(jnp.concatenate([cdd[q] * factor[:, q : q + 1] for q in range(step)], axis=1))
    lanes = pl.ds(pl.multiple_of(g * step * pair, step * pair), step * pair)
    chunk_hi, chunk_lo = u_hi[:, lanes], u_lo[:, lanes]
    right_terms[...] += nt(s_hi, chunk_hi) + nt(s_hi, chunk_lo) + nt(s_lo, chunk_hi)
    hi, lo = split(nn(rt_hi[...], s_hi) + nn(rt_hi[...], s_lo) + nn(rt_lo[...], s_hi))
    c_hi[:, lanes] = hi
    c_lo[:, lanes] = lo

    @pl.when(g == pl.num_programs(0) - 1)
    def _():
        t_hi, t_lo = split(left_t[...])
        t_both = jnp.concatenate([t_hi, t_lo], axis=0)
        left_grad[...] = jnp.zeros_like(left_grad)

        @pl.loop(0, width // 2)
        def _(q):
            def regroup(ref):
                cols = []
                for c in range(2):
                    at = pl.ds(pl.multiple_of((2 * q + c) * fam, fam), fam)
                    cols.append(
                        jnp.concatenate([ref[at, r * pair : (r + 1) * pair] for r in range(rows)], axis=0)
                    )
                return jnp.concatenate(cols, axis=1)

            hi, lo = regroup(c_hi), regroup(c_lo)
            lanes = pl.ds(pl.multiple_of(q * 2 * pair, 2 * pair), 2 * pair)
            w_hi, w_lo = split(weights[:, lanes])
            left_grad[...] += nt(hi, w_hi) + nt(hi, w_lo) + nt(lo, w_hi)
            both = nn(t_both, hi)
            out_grad[:, lanes] = both[:width] + both[width:] + nn(t_hi, lo)


def pair_work(cdd, masks, keep_rows, present_row, right, left, left_t, weights, fam):
    rows, total, pair = cdd.shape
    width = left.shape[1]
    step = keep_rows.shape[1]
    feats = width * fam
    whole = lambda a: pl.BlockSpec(a.shape, lambda g: (0,) * a.ndim)
    return pl.pallas_call(
        functools.partial(pair_kernel, step, fam),
        grid=(rows // step,),
        out_shape=(
            jax.ShapeDtypeStruct((total, feats), F32),
            jax.ShapeDtypeStruct((width, width * pair), F32),
            jax.ShapeDtypeStruct((rows * fam, width), F32),
        ),
        in_specs=[
            pl.BlockSpec((step, total, pair), lambda g: (g, 0, 0)),
            whole(masks),
            pl.BlockSpec((1,) + keep_rows.shape[1:], lambda g: (g, 0, 0)),
            pl.BlockSpec((1,) + present_row.shape[1:], lambda g: (g, 0, 0)),
            whole(right),
            whole(left),
            whole(left_t),
            whole(weights),
        ],
        out_specs=(
            pl.BlockSpec((total, feats), lambda g: (0, 0)),
            pl.BlockSpec((width, width * pair), lambda g: (0, 0)),
            pl.BlockSpec((rows * fam, width), lambda g: (0, 0)),
        ),
        scratch_shapes=[pltpu.VMEM((feats, total), BF16)] * 2 + [pltpu.VMEM((feats, rows * pair), BF16)] * 4,
        name="pair_work",
        compiler_params=pltpu.CompilerParams(vmem_limit_bytes=60 << 20, dimension_semantics=("arbitrary",)),
    )(cdd, masks, keep_rows, present_row, right, left, left_t, weights)


def local(n, act, valid, flags, w_left, w_right, w_final, cdd):
    rows, total, pair = cdd.shape
    fam, _, depth = act.shape
    width = w_left.shape[1]
    feats = width * fam
    half = n // 2
    keep = valid.astype(F32)
    present = flags.astype(F32)
    left = jnp.einsum("srm,ma->rsa", act, w_left, precision=EXACT) * keep.T[:, :, None]
    right = jnp.einsum("srm,mc->rcs", act, w_right, precision=EXACT) * keep.T[:, None, :]
    marks = jnp.concatenate([keep.T, present[:, None], jnp.zeros((rows, LANES - fam - 1), F32)], axis=1)
    block = jnp.concatenate([right.reshape(rows, feats), marks], axis=1)
    everyone = comm(gather_kernel, n, "gather_right", 0, (n, rows, feats + LANES), sems(half, half, n))(block)
    everyone = everyone.reshape(total, feats + LANES)

    step = min(4, rows)
    keep_rows = jnp.concatenate([keep.T, jnp.zeros((rows, LANES - fam), F32)], axis=1).reshape(-1, step, LANES)
    flat = left.reshape(rows * fam, width)
    right_terms, out_grad, left_grad = pair_work(
        cdd,
        everyone[:, feats:],
        keep_rows,
        present.reshape(-1, 1, step),
        everyone[:, :feats],
        flat,
        flat.T,
        w_final.reshape(width, width * pair),
        fam,
    )
    slab = pltpu.VMEM((half, rows, feats), F32)
    mine = comm(
        scatter_kernel, n, "scatter_right", 1, (rows, feats), [slab] * 3 + sems(half, half, half, half)
    )(right_terms.reshape(n, rows, feats))

    left_grad = left_grad.reshape(rows, fam, width) * keep.T[:, :, None]
    right_grad = mine.reshape(rows, width, fam) * keep.T[:, None, :]
    both = jnp.concatenate([left_grad.transpose(1, 0, 2), right_grad.transpose(2, 0, 1)], axis=2)
    w_both = jnp.concatenate([w_left, w_right], axis=1)
    alignment = jnp.einsum("srz,mz->srm", both, w_both, precision=EXACT)
    grads = jnp.einsum("srm,srz->mz", act, both, precision=EXACT)

    tail = 2 * depth * width // LANES
    used = width * width + tail
    piece = -(-used // (8 * n)) * 8
    packed = jnp.concatenate(
        [out_grad.reshape(width * width, pair), grads.reshape(tail, LANES), jnp.zeros((piece * n - used, LANES), F32)]
    )
    slab = pltpu.VMEM((half, piece, LANES), F32)
    summed = comm(
        reduce_kernel,
        n,
        "reduce_weights",
        2,
        (n, piece, LANES),
        [slab] * 3 + sems(half, half, half, half, half, half, n),
    )(packed.reshape(n, piece, LANES)).reshape(n * piece, LANES)
    grads = summed[width * width : used].reshape(depth, 2 * width)
    return alignment, grads[:, :width], grads[:, width:], summed[: width * width]


def solution(mesh):
    in_specs = (
        P("groups", "row", None),
        P("groups", "row"),
        P(("groups", "row")),
        P(),
        P(),
        P(),
        P(("groups", "row"), None, None),
    )
    out_specs = (P("groups", "row", None), P("groups", None), P("groups", None), P("groups", None))
    body = functools.partial(local, mesh.shape["row"])
    return jax.shard_map(body, mesh=mesh, in_specs=in_specs, out_specs=out_specs, check_vma=False)
```

```python
import functools

import jax
import jax.numpy as jnp
from jax import lax
from jax.experimental import pallas as pl
from jax.experimental.pallas import tpu as pltpu
from jax.sharding import PartitionSpec as P

F32, BF16 = jnp.float32, jnp.bfloat16
LANES = 128


def split(x):
    hi = x.astype(BF16)
    return hi, (x - hi.astype(F32)).astype(BF16)


def nn(a, b):
    return jnp.dot(a, b, preferred_element_type=F32)


def nt(a, b):
    return lax.dot_general(a, b, (((1,), (1,)), ((), ())), preferred_element_type=F32)


def remote(src, dst, send, recv, target):
    return pltpu.make_async_remote_copy(
        src_ref=src,
        dst_ref=dst,
        send_sem=send,
        recv_sem=recv,
        device_id={"row": target},
        device_id_type=pl.DeviceIdType.MESH,
    )


def each(start, stop, body):
    def one(k, _):
        body(k)
        return 0

    lax.fori_loop(start, stop, one, 0)


def sides(n):
    half, across = n // 2, 1
    while half % (2 * across) == 0 and 4 * across * across <= half:
        across *= 2
    return half // across, across


class Place:
    def __init__(self, n):
        self.n = n
        self.deep, self.wide = sides(n)
        self.me = lax.axis_index("row")
        self.core = lax.rem(self.me, 2)
        chip = lax.div(self.me, 2)
        self.x = lax.rem(chip, self.wide)
        self.z = lax.div(chip, self.wide)
        self.partner = self.at(0, 0, True)

    def at(self, k, m, other=False):
        z = lax.rem(self.z + k + self.deep, self.deep)
        x = lax.rem(self.x + m + self.wide, self.wide)
        core = 1 - self.core if other else self.core
        return (z * self.wide + x) * 2 + core

    def signal(self):
        barrier = pltpu.get_barrier_semaphore()

        def tell(target):
            pl.semaphore_signal(barrier, inc=1, device_id={"row": target}, device_id_type=pl.DeviceIdType.MESH)

        tell(self.partner)
        each(1, self.wide, lambda m: tell(self.at(0, m)))
        each(1, self.deep, lambda k: tell(self.at(k, 0)))

    def wait(self):
        pl.semaphore_wait(pltpu.get_barrier_semaphore(), self.deep + self.wide - 1)


class Gather:
    def __init__(self, place, own, out, z_send, x_send, c_send, recv):
        self.p, self.own, self.out = place, own, out
        self.z_send, self.x_send, self.c_send, self.recv = z_send, x_send, c_send, recv

    def copy(self, src, owner, send, target):
        return remote(src, self.out(owner), send, self.recv.at[owner], target)

    def start(self):
        p = self.p
        each(1, p.deep, lambda k: self.copy(self.own, p.me, self.z_send.at[k], p.at(k, 0)).start())
        each(1, p.wide, lambda m: self.copy(self.own, p.me, self.x_send.at[m], p.at(0, m)).start())
        self.copy(self.own, p.me, self.c_send.at[0], p.partner).start()

    def landed(self, owner):
        self.copy(self.out(owner), owner, self.z_send.at[0], self.p.partner).wait_recv()

    def cross(self):
        p = self.p

        def one(k):
            owner = p.at(-k, 0)
            self.landed(owner)
            block = self.out(owner)
            each(1, p.wide, lambda m: self.copy(block, owner, self.x_send.at[k * p.wide + m], p.at(0, m)).start())
            self.copy(block, owner, self.c_send.at[k * p.wide], p.partner).start()

        each(1, p.deep, one)

    def pair(self):
        p = self.p

        def one(k):
            def two(m):
                owner = p.at(-k, -m)
                self.landed(owner)
                self.copy(self.out(owner), owner, self.c_send.at[k * p.wide + m], p.partner).start()

            each(1, p.wide, two)

        each(0, p.deep, one)

    def finish(self):
        p = self.p
        each(0, p.deep, lambda k: each(0, p.wide, lambda m: self.landed(p.at(-k, -m, True))))

        def sent(sem):
            self.copy(self.own, p.me, sem, p.partner).wait_send()

        each(1, p.deep, lambda k: sent(self.z_send.at[k]))
        each(0, p.deep, lambda k: each(1, p.wide, lambda m: sent(self.x_send.at[k * p.wide + m])))
        each(0, p.deep * p.wide, lambda i: sent(self.c_send.at[i]))


class Scatter:
    def __init__(self, place, x, near, mid, far, staged, *sems):
        self.p, self.x, self.near, self.mid, self.far, self.staged = place, x, near, mid, far, staged
        self.near_send, self.near_recv, self.mid_send, self.mid_recv, self.far_send, self.far_recv = sems

    def near_copy(self, k, m):
        p, i = self.p, k * self.p.wide + m
        return remote(
            self.x(p.at(k, m, True)), self.near.at[i], self.near_send.at[i], self.near_recv.at[i], p.partner
        )

    def mid_copy(self, k, m):
        p, i = self.p, k * self.p.wide + m
        return remote(self.staged.at[i], self.mid.at[i], self.mid_send.at[i], self.mid_recv.at[i], p.at(0, m))

    def far_copy(self, k):
        p = self.p
        return remote(
            self.staged.at[k * p.wide], self.far.at[k], self.far_send.at[k], self.far_recv.at[k], p.at(k, 0)
        )

    def over(self, first, body):
        p = self.p
        each(0, p.deep, lambda k: each(first, p.wide, lambda m: body(k, m)))

    def start(self):
        self.over(1, lambda k, m: self.near_copy(k, m).start())
        each(0, self.p.deep, lambda k: self.near_copy(k, 0).start())

    def pair(self):
        p = self.p

        def merge(k, m):
            i = k * p.wide + m
            self.near_copy(k, m).wait_recv()
            self.staged[i] = self.x(p.at(k, m))[...] + self.near[i]

        def pass_on(k, m):
            merge(k, m)
            self.mid_copy(k, m).start()

        self.over(1, pass_on)
        each(0, p.deep, lambda k: merge(k, 0))

    def cross(self):
        p = self.p

        def merge(k):
            i = k * p.wide

            def one(m):
                self.mid_copy(k, m).wait_recv()
                self.staged[i] = self.staged[i] + self.mid[i + m]

            each(1, p.wide, one)

        def pass_on(k):
            merge(k)
            self.far_copy(k).start()

        each(1, p.deep, pass_on)
        merge(0)

    def finish(self):
        def one(k):
            self.far_copy(k).wait_recv()
            self.staged[0] = self.staged[0] + self.far[k]

        each(1, self.p.deep, one)
        self.over(0, lambda k, m: self.near_copy(k, m).wait_send())
        self.over(1, lambda k, m: self.mid_copy(k, m).wait_send())
        each(1, self.p.deep, lambda k: self.far_copy(k).wait_send())


def gather_sems(n):
    deep, wide = sides(n)
    return [pltpu.SemaphoreType.DMA((c,)) for c in (deep, deep * wide, deep * wide, n)]


def scatter_scratch(n, block):
    deep, wide = sides(n)
    most = deep * wide
    return [pltpu.VMEM((c,) + block, F32) for c in (most, most, deep, most)] + [
        pltpu.SemaphoreType.DMA((c,)) for c in (most, most, most, most, deep, deep)
    ]


def three(dot, a, b):
    a_hi, a_lo = split(a)
    b_hi, b_lo = split(b)
    return dot(a_hi, b_hi) + dot(a_hi, b_lo) + dot(a_lo, b_hi)


def kernel(
    n,
    step,
    fam,
    act,
    keep_t,
    marks,
    keep_rows,
    present_row,
    w_cat,
    w_final,
    cdd_hbm,
    align,
    left_w,
    right_w,
    out_w,
    *scratch,
):
    scratch = list(scratch)

    def take(count):
        taken = scratch[:count]
        del scratch[:count]
        return taken

    cdd, u, s_hi, s_lo, c_hi, c_lo, terms, terms_split = take(8)
    left, own_right, marks_all, right_all, flat_marks, turned, rt_hi, rt_lo, left_grad, both, packed, total_sum = take(12)
    (load,) = take(1)
    mark_sems, right_sems, sum_sems = take(4), take(4), take(4)
    right_scatter, sum_scatter = take(10), take(10)
    assert not scratch

    rows, total, pair = cdd.shape
    width = w_cat.shape[1] // 2
    groups = rows // step
    piece = packed.shape[0] // n
    place = Place(n)
    place.signal()

    def fetch(g):
        at = pl.ds(g * step, step)
        return pltpu.make_async_copy(cdd_hbm.at[at], cdd.at[at], load.at[g])

    each(0, groups, lambda g: fetch(g).start())

    projected = three(nn, act[...], w_cat[...])
    rights = []
    for s in range(fam):
        one = projected[s * rows : (s + 1) * rows] * keep_t[:, s : s + 1]
        rights.append(one[:, width:])
        left[pl.ds(s, rows, stride=fam), :] = jnp.concatenate([one, jnp.zeros((rows, LANES - 2 * width), F32)], axis=1)
    own_right[...] = jnp.concatenate(rights, axis=1)

    mark_gather = Gather(place, marks, lambda o: marks_all.at[o], *mark_sems)
    right_gather = Gather(place, own_right, lambda o: right_all.at[o], *right_sems)
    place.wait()
    mark_gather.start()
    right_gather.start()
    marks_all[place.me] = marks[...]
    right_all[place.me] = own_right[...]

    def weights(q):
        parts = [w_final[pl.ds(2 * q + b, width, stride=width), :] for b in range(2)]
        return jnp.concatenate(parts, axis=1)

    l_hi, l_lo = split(left[:, :width])
    l_three = jnp.concatenate([l_hi.astype(F32), l_hi.astype(F32), l_lo.astype(F32)], axis=1).astype(BF16)

    def make_u(q):
        w_hi, w_lo = split(weights(q))
        value = nn(l_three, jnp.concatenate([w_hi, w_lo, w_hi], axis=0))
        for b in range(2):
            for r in range(rows):
                u[r, pl.ds(2 * q + b, fam, stride=width), :] = value[
                    r * fam : (r + 1) * fam, b * pair : (b + 1) * pair
                ]

    each(0, width // 4, make_u)
    mark_gather.cross()
    each(width // 4, width // 2, make_u)
    mark_gather.pair()
    right_gather.cross()
    terms[...] = jnp.zeros_like(terms)
    mark_gather.finish()
    for o in range(n):
        flat_marks[o * rows : (o + 1) * rows, :] = marks_all[o]

    def lanes_of(g):
        return pl.ds(pl.multiple_of(g * step * pair, step * pair), step * pair)

    def make_terms(g):
        fetch(g).wait()
        count = nt(flat_marks[...].astype(BF16), keep_rows[g].astype(BF16))
        factor = flat_marks[:, fam : fam + 1] * present_row[g] / jnp.maximum(count, 1.0)
        hi, lo = split(jnp.concatenate([cdd[g * step + q] * factor[:, q : q + 1] for q in range(step)], axis=1))
        lanes = lanes_of(g)
        s_hi[:, lanes] = hi
        s_lo[:, lanes] = lo
        u_hi, u_lo = split(jnp.concatenate([u[g * step + q] for q in range(step)], axis=1))
        terms[...] += nt(hi, u_hi) + nt(hi, u_lo) + nt(lo, u_hi)

    each(0, groups // 4, make_terms)
    right_gather.pair()
    each(groups // 4, groups, make_terms)
    right_gather.finish()

    for o in range(n):
        terms_split[o] = terms[o * rows : (o + 1) * rows, :]
    right_sum = Scatter(place, lambda o: terms_split.at[o], *right_scatter)
    right_sum.start()
    for o in range(n):
        terms[o * rows : (o + 1) * rows, :] = right_all[o]
    for t in range(total // LANES):
        at = slice(t * LANES, (t + 1) * LANES)
        turned[t] = terms[at, :].T
        for c in range(width):
            hi, lo = split(turned[t, pl.ds(c, fam, stride=width), :])
            rt_hi[c * fam : (c + 1) * fam, at] = hi
            rt_lo[c * fam : (c + 1) * fam, at] = lo

    def make_carried(g):
        lanes = lanes_of(g)
        hi, lo = split(
            nn(rt_hi[...], s_hi[:, lanes]) + nn(rt_hi[...], s_lo[:, lanes]) + nn(rt_lo[...], s_hi[:, lanes])
        )
        c_hi[:, lanes] = hi
        c_lo[:, lanes] = lo

    each(0, groups // 4, make_carried)
    right_sum.pair()
    each(groups // 4, 3 * groups // 4, make_carried)
    right_sum.cross()
    each(3 * groups // 4, groups, make_carried)

    t_hi, t_lo = split(left[...].T[:width])
    t_both = jnp.concatenate([t_hi, t_lo], axis=0)
    left_grad[...] = jnp.zeros_like(left_grad)

    def contract(q):
        def regroup(ref):
            cols = []
            for c in range(2):
                at = pl.ds(pl.multiple_of((2 * q + c) * fam, fam), fam)
                cols.append(jnp.concatenate([ref[at, r * pair : (r + 1) * pair] for r in range(rows)], axis=0))
            return jnp.concatenate(cols, axis=1)

        hi, lo = regroup(c_hi), regroup(c_lo)
        w_hi, w_lo = split(weights(q))
        left_grad[:, :width] += nt(hi, w_hi) + nt(hi, w_lo) + nt(lo, w_hi)
        two = nn(t_both, hi)
        value = two[:width] + two[width:] + nn(t_hi, lo)
        for c in range(2):
            at = pl.ds(pl.multiple_of((2 * q + c) * width, width), width)
            packed[at, :] = value[:, c * pair : (c + 1) * pair]

    each(0, width // 2, contract)
    right_sum.finish()

    mine = right_scatter[3]
    for s in range(fam):
        one = jnp.concatenate(
            [left_grad[pl.ds(s, rows, stride=fam), :][:, :width], mine[0, :, s * width : (s + 1) * width]], axis=1
        )
        both[s * rows : (s + 1) * rows, :] = jnp.concatenate(
            [one * keep_t[:, s : s + 1], jnp.zeros((rows, LANES - 2 * width), F32)], axis=1
        )
    grads = three(nn, both[...].T, act[...])[: 2 * width]
    base = width * width
    tiles = act.shape[1] // LANES
    for t in range(tiles):
        packed[base + t * 2 * width : base + (t + 1) * 2 * width, :] = grads[:, t * LANES : (t + 1) * LANES]
    end = base + tiles * 2 * width
    if end < packed.shape[0]:
        packed[end:, :] = jnp.zeros((packed.shape[0] - end, LANES), F32)

    def piece_of(ref):
        return lambda o: ref.at[pl.ds(pl.multiple_of(o * piece, 8), piece), :]

    weight_sum = Scatter(place, piece_of(packed), *sum_scatter)
    weight_sum.start()
    align[...] = three(nt, both[:, : 2 * width], w_cat[...])
    weight_sum.pair()
    weight_sum.cross()
    weight_sum.finish()
    summed = sum_scatter[3]
    spread = Gather(place, summed.at[0], piece_of(total_sum), *sum_sems)
    spread.start()
    total_sum[pl.ds(pl.multiple_of(place.me * piece, 8), piece), :] = summed[0]
    spread.cross()
    spread.pair()
    spread.finish()

    for c in range(width):
        out_w[pl.ds(c, width, stride=width), :] = total_sum[c * width : (c + 1) * width, :]
    for t in range(tiles):
        at = slice(t * LANES, (t + 1) * LANES)
        part = total_sum[base + t * 2 * width : base + (t + 1) * 2 * width, :]
        part = jnp.concatenate([part, jnp.zeros((LANES - 2 * width, LANES), F32)], axis=0).T
        left_w[at, :] = part[:, :width]
        right_w[at, :] = part[:, width : 2 * width]


def local(n, act, valid, flags, w_left, w_right, w_final, cdd):
    rows, total, pair = cdd.shape
    fam, _, depth = act.shape
    width = w_left.shape[1]
    feats = width * fam
    keep_t = valid.astype(F32).T
    present = flags.astype(F32)
    marks = jnp.concatenate([keep_t, present[:, None], jnp.zeros((rows, LANES - fam - 1), F32)], axis=1)
    step = min(4, rows)
    keep_rows = jnp.concatenate([keep_t, jnp.zeros((rows, LANES - fam), F32)], axis=1).reshape(-1, step, LANES)
    used = width * width + 2 * depth * width // LANES
    piece = -(-used // (8 * n)) * 8
    vm = pl.BlockSpec(memory_space=pltpu.VMEM)
    f32 = lambda *shape: pltpu.VMEM(shape, F32)
    b16 = lambda *shape: pltpu.VMEM(shape, BF16)
    align, left_w, right_w, out_w = pl.pallas_call(
        functools.partial(kernel, n, step, fam),
        out_shape=tuple(
            jax.ShapeDtypeStruct(shape, F32)
            for shape in ((fam * rows, depth), (depth, width), (depth, width), (width * width, pair))
        ),
        in_specs=[vm] * 7 + [pl.BlockSpec(memory_space=pl.ANY)],
        out_specs=(vm,) * 4,
        scratch_shapes=[
            f32(rows, total, pair),
            f32(rows, feats, pair),
            b16(total, rows * pair),
            b16(total, rows * pair),
            b16(feats, rows * pair),
            b16(feats, rows * pair),
            f32(total, feats),
            f32(n, rows, feats),
            f32(rows * fam, LANES),
            f32(rows, feats),
            f32(n, rows, LANES),
            f32(n, rows, feats),
            f32(total, LANES),
            f32(total // LANES, feats, LANES),
            b16(feats, total),
            b16(feats, total),
            f32(rows * fam, LANES),
            f32(fam * rows, LANES),
            f32(n * piece, LANES),
            f32(n * piece, LANES),
            pltpu.SemaphoreType.DMA((rows // step,)),
        ]
        + gather_sems(n) * 3
        + scatter_scratch(n, (rows, feats))
        + scatter_scratch(n, (piece, LANES)),
        name="outer_mean_grad",
        compiler_params=pltpu.CompilerParams(collective_id=0, has_side_effects=True, vmem_limit_bytes=60 << 20),
    )(
        act.reshape(fam * rows, depth),
        keep_t,
        marks,
        keep_rows,
        present.reshape(-1, 1, step),
        jnp.concatenate([w_left, w_right], axis=1),
        w_final,
        cdd,
    )
    return align.reshape(fam, rows, depth), left_w, right_w, out_w


def solution(mesh):
    in_specs = (
        P("groups", "row", None),
        P("groups", "row"),
        P(("groups", "row")),
        P(),
        P(),
        P(),
        P(("groups", "row"), None, None),
    )
    out_specs = (P("groups", "row", None), P("groups", None), P("groups", None), P("groups", None))
    body = functools.partial(local, mesh.shape["row"])
    return jax.shard_map(body, mesh=mesh, in_specs=in_specs, out_specs=out_specs, check_vma=False)
```

```python
import functools

import jax
import jax.numpy as jnp
from jax import lax
from jax.experimental import pallas as pl
from jax.experimental.pallas import tpu as pltpu
from jax.sharding import PartitionSpec as P

F32, BF16 = jnp.float32, jnp.bfloat16
LANES = 128


def split(x):
    hi = x.astype(BF16)
    return hi, (x - hi.astype(F32)).astype(BF16)


def nn(a, b):
    return jnp.dot(a, b, preferred_element_type=F32)


def nt(a, b):
    return lax.dot_general(a, b, (((1,), (1,)), ((), ())), preferred_element_type=F32)


def remote(src, dst, send, recv, target):
    return pltpu.make_async_remote_copy(
        src_ref=src,
        dst_ref=dst,
        send_sem=send,
        recv_sem=recv,
        device_id={"row": target},
        device_id_type=pl.DeviceIdType.MESH,
    )


def each(start, stop, body):
    def one(k, _):
        body(k)
        return 0

    lax.fori_loop(start, stop, one, 0)


def sides(n):
    half, across = n // 2, 1
    while half % (2 * across) == 0 and 4 * across * across <= half:
        across *= 2
    return half // across, across


class Place:
    def __init__(self, n):
        self.n = n
        self.deep, self.wide = sides(n)
        self.me = lax.axis_index("row")
        self.core = lax.rem(self.me, 2)
        chip = lax.div(self.me, 2)
        self.x = lax.rem(chip, self.wide)
        self.z = lax.div(chip, self.wide)
        self.partner = self.at(0, 0, True)

    def at(self, k, m, other=False):
        z = lax.rem(self.z + k + self.deep, self.deep)
        x = lax.rem(self.x + m + self.wide, self.wide)
        core = 1 - self.core if other else self.core
        return (z * self.wide + x) * 2 + core

    def signal(self):
        barrier = pltpu.get_barrier_semaphore()

        def tell(target):
            pl.semaphore_signal(barrier, inc=1, device_id={"row": target}, device_id_type=pl.DeviceIdType.MESH)

        tell(self.partner)
        each(1, self.wide, lambda m: tell(self.at(0, m)))
        each(1, self.deep, lambda k: tell(self.at(k, 0)))

    def wait(self):
        pl.semaphore_wait(pltpu.get_barrier_semaphore(), self.deep + self.wide - 1)


class Gather:
    def __init__(self, place, own, out, z_send, x_send, c_send, recv):
        self.p, self.own, self.out = place, own, out
        self.z_send, self.x_send, self.c_send, self.recv = z_send, x_send, c_send, recv

    def copy(self, src, owner, send, target):
        return remote(src, self.out(owner), send, self.recv.at[owner], target)

    def start(self):
        p = self.p
        each(1, p.deep, lambda k: self.copy(self.own, p.me, self.z_send.at[k], p.at(k, 0)).start())
        each(1, p.wide, lambda m: self.copy(self.own, p.me, self.x_send.at[m], p.at(0, m)).start())
        self.copy(self.own, p.me, self.c_send.at[0], p.partner).start()

    def landed(self, owner):
        self.copy(self.out(owner), owner, self.z_send.at[0], self.p.partner).wait_recv()

    def cross(self):
        p = self.p

        def one(k):
            owner = p.at(-k, 0)
            self.landed(owner)
            block = self.out(owner)
            each(1, p.wide, lambda m: self.copy(block, owner, self.x_send.at[k * p.wide + m], p.at(0, m)).start())
            self.copy(block, owner, self.c_send.at[k * p.wide], p.partner).start()

        each(1, p.deep, one)

    def pair(self):
        p = self.p

        def one(k):
            def two(m):
                owner = p.at(-k, -m)
                self.landed(owner)
                self.copy(self.out(owner), owner, self.c_send.at[k * p.wide + m], p.partner).start()

            each(1, p.wide, two)

        each(0, p.deep, one)

    def finish(self):
        p = self.p
        each(0, p.deep, lambda k: each(0, p.wide, lambda m: self.landed(p.at(-k, -m, True))))

        def sent(sem):
            self.copy(self.own, p.me, sem, p.partner).wait_send()

        each(1, p.deep, lambda k: sent(self.z_send.at[k]))
        each(0, p.deep, lambda k: each(1, p.wide, lambda m: sent(self.x_send.at[k * p.wide + m])))
        each(0, p.deep * p.wide, lambda i: sent(self.c_send.at[i]))


class Scatter:
    def __init__(self, place, x, near, mid, far, staged, *sems):
        self.p, self.x, self.near, self.mid, self.far, self.staged = place, x, near, mid, far, staged
        self.near_send, self.near_recv, self.mid_send, self.mid_recv, self.far_send, self.far_recv = sems

    def near_copy(self, k, m):
        p, i = self.p, k * self.p.wide + m
        return remote(
            self.x(p.at(k, m, True)), self.near.at[i], self.near_send.at[i], self.near_recv.at[i], p.partner
        )

    def mid_copy(self, k, m):
        p, i = self.p, k * self.p.wide + m
        return remote(self.staged.at[i], self.mid.at[i], self.mid_send.at[i], self.mid_recv.at[i], p.at(0, m))

    def far_copy(self, k):
        p = self.p
        return remote(
            self.staged.at[k * p.wide], self.far.at[k], self.far_send.at[k], self.far_recv.at[k], p.at(k, 0)
        )

    def over(self, first, body):
        p = self.p
        each(0, p.deep, lambda k: each(first, p.wide, lambda m: body(k, m)))

    def start(self):
        self.over(1, lambda k, m: self.near_copy(k, m).start())
        each(0, self.p.deep, lambda k: self.near_copy(k, 0).start())

    def pair(self):
        p = self.p

        def merge(k, m):
            i = k * p.wide + m
            self.near_copy(k, m).wait_recv()
            self.staged[i] = self.x(p.at(k, m))[...] + self.near[i]

        def pass_on(k, m):
            merge(k, m)
            self.mid_copy(k, m).start()

        self.over(1, pass_on)
        each(0, p.deep, lambda k: merge(k, 0))

    def cross(self):
        p = self.p

        def merge(k):
            i = k * p.wide

            def one(m):
                self.mid_copy(k, m).wait_recv()
                self.staged[i] = self.staged[i] + self.mid[i + m]

            each(1, p.wide, one)

        def pass_on(k):
            merge(k)
            self.far_copy(k).start()

        each(1, p.deep, pass_on)
        merge(0)

    def finish(self):
        def one(k):
            self.far_copy(k).wait_recv()
            self.staged[0] = self.staged[0] + self.far[k]

        each(1, self.p.deep, one)
        self.over(0, lambda k, m: self.near_copy(k, m).wait_send())
        self.over(1, lambda k, m: self.mid_copy(k, m).wait_send())
        each(1, self.p.deep, lambda k: self.far_copy(k).wait_send())


def gather_sems(n):
    deep, wide = sides(n)
    return [pltpu.SemaphoreType.DMA((c,)) for c in (deep, deep * wide, deep * wide, n)]


def scatter_scratch(n, block):
    deep, wide = sides(n)
    most = deep * wide
    return [pltpu.VMEM((c,) + block, F32) for c in (most, most, deep, most)] + [
        pltpu.SemaphoreType.DMA((c,)) for c in (most, most, most, most, deep, deep)
    ]


def three(dot, a, b):
    a_hi, a_lo = split(a)
    b_hi, b_lo = split(b)
    return dot(a_hi, b_hi) + dot(a_hi, b_lo) + dot(a_lo, b_hi)


def kernel(
    n,
    step,
    fam,
    act,
    valid,
    flags,
    w_left,
    w_right,
    w_final,
    cdd_hbm,
    align,
    total_sum,
    *scratch,
):
    scratch = list(scratch)

    def take(count):
        taken = scratch[:count]
        del scratch[:count]
        return taken

    cdd, u, s_hi, s_lo, c_hi, c_lo, terms, terms_split = take(8)
    left, own_right, marks_all, right_all, flat_marks, turned, rt_hi, rt_lo, left_grad, both, packed = take(11)
    board, marks, keep_rows, present_row = take(4)
    (load,) = take(1)
    mark_sems, right_sems, sum_sems = take(4), take(4), take(4)
    right_scatter, sum_scatter = take(10), take(10)
    assert not scratch

    rows, total, pair = cdd.shape
    width = w_left.shape[0]
    groups = rows // step
    piece = packed.shape[0] // n
    place = Place(n)
    place.signal()

    def fetch(g):
        at = pl.ds(g * step, step)
        return pltpu.make_async_copy(cdd_hbm.at[at], cdd.at[at], load.at[g])

    each(0, groups, lambda g: fetch(g).start())

    board[...] = jnp.zeros_like(board)
    board[:fam, :rows] = valid[...].astype(F32)
    board[fam : fam + 1, :rows] = flags[...].astype(F32)
    marks[...] = board[...].T[:rows]
    keep_t = marks[:, :fam]
    lane = lax.broadcasted_iota(jnp.int32, (rows, LANES), 1)
    kept = jnp.where(lane < fam, marks[...], 0.0)
    for g in range(groups):
        keep_rows[g] = kept[g * step : (g + 1) * step]
        present_row[g] = board[fam : fam + 1, g * step : (g + 1) * step]

    w_cat = jnp.concatenate([w_left[...], w_right[...]], axis=0)
    projected = three(nt, act[...], w_cat)
    rights = []
    for s in range(fam):
        one = projected[s * rows : (s + 1) * rows] * keep_t[:, s : s + 1]
        rights.append(one[:, width:])
        left[pl.ds(s, rows, stride=fam), :] = jnp.concatenate([one, jnp.zeros((rows, LANES - 2 * width), F32)], axis=1)
    own_right[...] = jnp.concatenate(rights, axis=1)

    mark_gather = Gather(place, marks, lambda o: marks_all.at[o], *mark_sems)
    right_gather = Gather(place, own_right, lambda o: right_all.at[o], *right_sems)
    place.wait()
    mark_gather.start()
    right_gather.start()
    marks_all[place.me] = marks[...]
    right_all[place.me] = own_right[...]

    def weights(q):
        parts = [w_final[pl.ds(2 * q + b, width, stride=width), :] for b in range(2)]
        return jnp.concatenate(parts, axis=1)

    l_hi, l_lo = split(left[:, :width])
    l_three = jnp.concatenate([l_hi.astype(F32), l_hi.astype(F32), l_lo.astype(F32)], axis=1).astype(BF16)

    def make_u(q):
        w_hi, w_lo = split(weights(q))
        value = nn(l_three, jnp.concatenate([w_hi, w_lo, w_hi], axis=0))
        for b in range(2):
            for r in range(rows):
                u[r, pl.ds(2 * q + b, fam, stride=width), :] = value[
                    r * fam : (r + 1) * fam, b * pair : (b + 1) * pair
                ]

    each(0, width // 4, make_u)
    mark_gather.cross()
    each(width // 4, width // 2, make_u)
    mark_gather.pair()
    right_gather.cross()
    terms[...] = jnp.zeros_like(terms)
    mark_gather.finish()
    for o in range(n):
        flat_marks[o * rows : (o + 1) * rows, :] = marks_all[o]

    def lanes_of(g):
        return pl.ds(pl.multiple_of(g * step * pair, step * pair), step * pair)

    def make_terms(g):
        fetch(g).wait()
        count = nt(flat_marks[...].astype(BF16), keep_rows[g].astype(BF16))
        factor = flat_marks[:, fam : fam + 1] * present_row[g] / jnp.maximum(count, 1.0)
        hi, lo = split(jnp.concatenate([cdd[g * step + q] * factor[:, q : q + 1] for q in range(step)], axis=1))
        lanes = lanes_of(g)
        s_hi[:, lanes] = hi
        s_lo[:, lanes] = lo
        u_hi, u_lo = split(jnp.concatenate([u[g * step + q] for q in range(step)], axis=1))
        terms[...] += nt(hi, u_hi) + nt(hi, u_lo) + nt(lo, u_hi)

    each(0, groups // 4, make_terms)
    right_gather.pair()
    each(groups // 4, groups, make_terms)
    right_gather.finish()

    for o in range(n):
        terms_split[o] = terms[o * rows : (o + 1) * rows, :]
    right_sum = Scatter(place, lambda o: terms_split.at[o], *right_scatter)
    right_sum.start()
    for o in range(n):
        terms[o * rows : (o + 1) * rows, :] = right_all[o]
    for t in range(total // LANES):
        at = slice(t * LANES, (t + 1) * LANES)
        turned[t] = terms[at, :].T
        for c in range(width):
            hi, lo = split(turned[t, pl.ds(c, fam, stride=width), :])
            rt_hi[c * fam : (c + 1) * fam, at] = hi
            rt_lo[c * fam : (c + 1) * fam, at] = lo

    def make_carried(g):
        lanes = lanes_of(g)
        hi, lo = split(
            nn(rt_hi[...], s_hi[:, lanes]) + nn(rt_hi[...], s_lo[:, lanes]) + nn(rt_lo[...], s_hi[:, lanes])
        )
        c_hi[:, lanes] = hi
        c_lo[:, lanes] = lo

    each(0, groups // 4, make_carried)
    right_sum.pair()
    each(groups // 4, 3 * groups // 4, make_carried)
    right_sum.cross()
    each(3 * groups // 4, groups, make_carried)

    t_hi, t_lo = split(left[...].T[:width])
    t_both = jnp.concatenate([t_hi, t_lo], axis=0)
    left_grad[...] = jnp.zeros_like(left_grad)

    def contract(q):
        def regroup(ref):
            cols = []
            for c in range(2):
                at = pl.ds(pl.multiple_of((2 * q + c) * fam, fam), fam)
                cols.append(jnp.concatenate([ref[at, r * pair : (r + 1) * pair] for r in range(rows)], axis=0))
            return jnp.concatenate(cols, axis=1)

        hi, lo = regroup(c_hi), regroup(c_lo)
        w_hi, w_lo = split(weights(q))
        left_grad[:, :width] += nt(hi, w_hi) + nt(hi, w_lo) + nt(lo, w_hi)
        two = nn(t_both, hi)
        value = two[:width] + two[width:] + nn(t_hi, lo)
        for c in range(2):
            at = pl.ds(pl.multiple_of((2 * q + c) * width, width), width)
            packed[at, :] = value[:, c * pair : (c + 1) * pair]

    each(0, width // 2, contract)
    right_sum.finish()

    mine = right_scatter[3]
    for s in range(fam):
        one = jnp.concatenate(
            [left_grad[pl.ds(s, rows, stride=fam), :][:, :width], mine[0, :, s * width : (s + 1) * width]], axis=1
        )
        both[s * rows : (s + 1) * rows, :] = jnp.concatenate(
            [one * keep_t[:, s : s + 1], jnp.zeros((rows, LANES - 2 * width), F32)], axis=1
        )
    grads = three(nn, both[...].T, act[...])[: 2 * width]
    base = width * width
    tiles = act.shape[1] // LANES
    for t in range(tiles):
        packed[base + t * 2 * width : base + (t + 1) * 2 * width, :] = grads[:, t * LANES : (t + 1) * LANES]
    end = base + tiles * 2 * width
    if end < packed.shape[0]:
        packed[end:, :] = jnp.zeros((packed.shape[0] - end, LANES), F32)

    def piece_of(ref):
        return lambda o: ref.at[pl.ds(pl.multiple_of(o * piece, 8), piece), :]

    weight_sum = Scatter(place, piece_of(packed), *sum_scatter)
    weight_sum.start()
    align[...] = three(nn, both[:, : 2 * width], w_cat)
    weight_sum.pair()
    weight_sum.cross()
    weight_sum.finish()
    summed = sum_scatter[3]
    spread = Gather(place, summed.at[0], piece_of(total_sum), *sum_sems)
    spread.start()
    total_sum[pl.ds(pl.multiple_of(place.me * piece, 8), piece), :] = summed[0]
    spread.cross()
    spread.pair()
    spread.finish()


def unpack_kernel(align, total_sum, align_out, left_w, right_w, out_w):
    width, depth = left_w.shape
    base = width * width
    align_out[...] = align[...]
    for c in range(width):
        out_w[pl.ds(c, width, stride=width), :] = total_sum[c * width : (c + 1) * width, :]
    for t in range(depth // LANES):
        at = slice(t * LANES, (t + 1) * LANES)
        first = base + t * 2 * width
        left_w[:, at] = total_sum[first : first + width, :]
        right_w[:, at] = total_sum[first + width : first + 2 * width, :]


def local(n, act, valid, flags, w_left, w_right, w_final, cdd):
    rows, total, pair = cdd.shape
    fam, _, depth = act.shape
    width = w_left.shape[1]
    feats = width * fam
    step = min(4, rows)
    used = width * width + 2 * depth * width // LANES
    piece = -(-used // (8 * n)) * 8
    vm = pl.BlockSpec(memory_space=pltpu.VMEM)
    f32 = lambda *shape: pltpu.VMEM(shape, F32)
    b16 = lambda *shape: pltpu.VMEM(shape, BF16)
    align, total_sum = pl.pallas_call(
        functools.partial(kernel, n, step, fam),
        out_shape=tuple(
            jax.ShapeDtypeStruct(shape, F32)
            for shape in ((fam * rows, depth), (n * piece, LANES))
        ),
        in_specs=[vm] * 6 + [pl.BlockSpec(memory_space=pl.ANY)],
        out_specs=(vm,) * 2,
        scratch_shapes=[
            f32(rows, total, pair),
            f32(rows, feats, pair),
            b16(total, rows * pair),
            b16(total, rows * pair),
            b16(feats, rows * pair),
            b16(feats, rows * pair),
            f32(total, feats),
            f32(n, rows, feats),
            f32(rows * fam, LANES),
            f32(rows, feats),
            f32(n, rows, LANES),
            f32(n, rows, feats),
            f32(total, LANES),
            f32(total // LANES, feats, LANES),
            b16(feats, total),
            b16(feats, total),
            f32(rows * fam, LANES),
            f32(fam * rows, LANES),
            f32(n * piece, LANES),
            f32(LANES, LANES),
            f32(rows, LANES),
            f32(rows // step, step, LANES),
            f32(rows // step, 1, step),
            pltpu.SemaphoreType.DMA((rows // step,)),
        ]
        + gather_sems(n) * 3
        + scatter_scratch(n, (rows, feats))
        + scatter_scratch(n, (piece, LANES)),
        name="outer_mean_grad",
        compiler_params=pltpu.CompilerParams(collective_id=0, has_side_effects=True, vmem_limit_bytes=60 << 20),
    )(
        act.reshape(fam * rows, depth),
        valid,
        flags.reshape(1, rows),
        w_left.T,
        w_right.T,
        w_final,
        cdd,
    )
    align, left_w, right_w, out_w = pl.pallas_call(
        unpack_kernel,
        out_shape=tuple(
            jax.ShapeDtypeStruct(shape, F32)
            for shape in ((fam * rows, depth), (width, depth), (width, depth), (width * width, pair))
        ),
        in_specs=[vm] * 2,
        out_specs=(vm,) * 4,
        name="unpack",
    )(align, total_sum)
    return align.reshape(fam, rows, depth), left_w.T, right_w.T, out_w


def solution(mesh):
    in_specs = (
        P("groups", "row", None),
        P("groups", "row"),
        P(("groups", "row")),
        P(),
        P(),
        P(),
        P(("groups", "row"), None, None),
    )
    out_specs = (P("groups", "row", None), P("groups", None), P("groups", None), P("groups", None))
    body = functools.partial(local, mesh.shape["row"])
    return jax.shard_map(body, mesh=mesh, in_specs=in_specs, out_specs=out_specs, check_vma=False)
```
